32 devices in a mesh: groups: 2 (over y), blk: 4 (over z), cols: 2 (over x), sub: 2 (over core).
Axes of the slice: x: 2, y: 2, z: 4, core: 2. Of those that a mesh axis runs over, the one named last changes fastest.
Arguments:
- features: bfloat16 [4096, 256], P(('groups', 'blk', 'cols'), 'sub'), parts along dimension 0, may hold values from -60 to 60, as said below
- vector: float32 [4096], P(('groups', 'blk', 'cols')), parts along dimension 0, may hold values from 0.1 to 100, as said below
Outputs:
- new_vector: float32 [4096], P(('groups', 'blk', 'cols')), parts along dimension 0
- mean_affinity: float32 [4096], P(('groups', 'blk', 'cols')), parts along dimension 0
The draws below stay inside these ranges and needn't reach their ends.
There are 2 independent parts, one for each index of `groups`. The reference program is written for one: setup_inputs(seed, part) draws one part's arguments, and reference() takes and returns one part's arrays. A program takes and returns all parts, laid end to end along the dimension named above; each array names one. Nothing has to cross between parts.
Inputs may be any that keep to these rules, and one draw needn't show every extreme that they name: Real-valued features; no row is zero. `vector`: positive entries.
All inputs are finite; a program needn't handle non-finite values. Where the reference program divides by a largest or mean magnitude, that divisor is 1e-20 or more.
Results may differ from the reference program's by a relative error of at most 0.0033.
Values may be sent and summed in bfloat16 or wider, within the bound.
A program may use at most 64 MiB of HBM per device.

```python
import math
import jax
import jax.numpy as jnp
from jax import lax

F = 256
POWER = 16
POINTS = 2048
CLUSTERS = 64


def draw_features(key, part):
    base = jax.random.fold_in(key, 7)
    key_ids = jax.random.fold_in(base, 0)
    key_centers = jax.random.fold_in(base, 1)
    key_noise = jax.random.fold_in(base, 2)
    key_kind = jax.random.fold_in(base, 4)
    half_count = max(CLUSTERS // 2, 1)
    global_labels = jax.random.randint(key_ids, (POINTS,), 0, half_count)
    positions = jnp.arange(POINTS, dtype=jnp.int32)
    local_labels = CLUSTERS - half_count + positions * half_count // POINTS
    local_labels = jnp.minimum(local_labels, CLUSTERS - 1)
    kind = jax.random.randint(key_kind, (POINTS,), 0, 2)
    labels = jnp.where(kind == 1, local_labels, global_labels)
    centers = jnp.clip(jax.random.normal(key_centers, (CLUSTERS, F), jnp.float32), -4.0, 4.0)
    chosen = centers[labels]
    noise = 0.5 * jnp.clip(jax.random.normal(key_noise, (POINTS, F), jnp.float32), -4.0, 4.0)
    return (chosen + noise).astype(jnp.bfloat16)


def draw_vector(key, part):
    base = jax.random.fold_in(key, 11)
    rising = jnp.arange(POINTS, dtype=jnp.float32) / POINTS
    factor = jnp.exp(jax.random.uniform(base, (POINTS,), jnp.float32, jnp.log(0.1), jnp.log(10.0)))
    return factor * jnp.exp(jnp.log(10.0) * rising)


def setup_inputs(seed: int = 0, part: int = 0) -> dict:
    arg_keys = jax.random.split(jax.random.key(seed), 3)
    part_splits = jax.random.split(jax.random.fold_in(arg_keys[2], part), 3)
    return {
        "features": draw_features(jax.random.fold_in(jax.random.fold_in(arg_keys[2], part), 71), part),
        "vector": draw_vector(jax.random.fold_in(jax.random.fold_in(arg_keys[2], part), 71), part),
    }


def reference(features, vector):
    widened = features.astype(jnp.float32)
    unit_rows = (widened * lax.rsqrt(lax.optimization_barrier(jnp.mean(widened * widened, axis=1, keepdims=True)) + 1e-06) * (1.0 / math.sqrt(F))).astype(jnp.bfloat16)
    all_unit = unit_rows.astype(jnp.float32)
    block_len = math.gcd(POINTS, 512)
    blocks = POINTS // block_len
    stacked = all_unit.reshape(blocks, block_len, F)
    squarings = POWER.bit_length() - 1

    def one_block(block_rows):
        cosine = jnp.dot(block_rows, all_unit.T, precision=lax.Precision.HIGHEST)
        affinity = (1.0 + cosine) * 0.5
        for level in range(squarings):
            affinity = affinity * affinity
        weighted = jnp.dot(affinity, vector, precision=lax.Precision.HIGHEST)
        return (weighted, lax.optimization_barrier(jnp.sum(affinity, axis=1)))
    weighted, degree = lax.map(one_block, stacked)
    weighted = weighted.reshape(POINTS)
    degree = degree.reshape(POINTS)
    averaged = weighted / degree
    mean_abs = jnp.mean(jnp.abs(averaged)) + 1e-06
    return (averaged / mean_abs, degree / POINTS)
```

```python
import functools
import math

import jax
import jax.numpy as jnp
from jax import lax
from jax.experimental import pallas as pl
from jax.experimental.pallas import tpu as pltpu
from jax.sharding import PartitionSpec as P

POWER = 16
MESH = pl.DeviceIdType.MESH


def normalize(first, second):
    first = first.astype(jnp.float32)
    second = second.astype(jnp.float32)
    width = first.shape[1] + second.shape[1]
    squares = jnp.sum(first * first + second * second, axis=1, keepdims=True)
    scale = lax.rsqrt(squares * (1.0 / width) + 1e-06) * (1.0 / math.sqrt(width))
    return (first * scale).astype(jnp.bfloat16), (second * scale).astype(jnp.bfloat16)


def kernel(
    nb, nc, ns, f_ref, v_ref, new_ref, mean_ref,
    row_buf, col_buf, val_buf, unit, part, red_buf, tot, tot_buf,
    row_send, row_recv, col_send, col_recv, val_send, val_recv,
    red_send, red_recv, tot_send, tot_recv,
):
    z, x, c = lax.axis_index("blk"), lax.axis_index("cols"), lax.axis_index("sub")
    rows, feats = f_ref.shape
    half = rows // ns
    points = rows * nb * nc
    plane = [(d, e) for d in range(nc) for e in range(ns) if (d, e) != (0, 0)]
    ahead = list(range(1, nb))

    def plane_id(d, e):
        return {"cols": lax.rem(x + d, nc), "sub": lax.rem(c + e, ns)}

    def line_id(d, e):
        return {"blk": lax.rem(z + d, nb), "sub": lax.rem(c + e, ns)}

    barrier = pltpu.get_barrier_semaphore()
    for d in ahead:
        for e in range(ns):
            pl.semaphore_signal(barrier, 1, device_id=line_id(d, e), device_id_type=MESH)
    for d, e in plane:
        pl.semaphore_signal(barrier, 1, device_id=plane_id(d, e), device_id_type=MESH)
    pl.semaphore_wait(barrier, len(plane) + len(ahead) * ns)

    def remote(src, dst, send, recv, device):
        copy = pltpu.make_async_remote_copy(
            src_ref=src, dst_ref=dst, send_sem=send, recv_sem=recv,
            device_id=device, device_id_type=MESH,
        )
        copy.start()
        return copy

    row_copy, col_copy, val_copy, red_copy, tot_copy = {}, {}, {}, {}, {}
    own = pl.ds(pl.multiple_of(c * half, half), half)
    for d, e in plane:
        slot = ((nc - d) % nc, e)
        row_copy[slot] = remote(
            f_ref, row_buf.at[slot], row_send.at[slot], row_recv.at[slot], plane_id(d, e)
        )
    for d in ahead:
        val_copy[nb - d] = remote(
            v_ref.at[:, own], val_buf.at[nb - d], val_send.at[nb - d], val_recv.at[nb - d],
            line_id(d, 0),
        )
        for e in range(ns):
            slot = (nb - d, e)
            wanted = pl.ds(pl.multiple_of(lax.rem(c + e, ns) * half, half), half)
            col_copy[slot] = remote(
                f_ref.at[wanted, :], col_buf.at[slot], col_send.at[slot], col_recv.at[slot],
                line_id(d, e),
            )

    for d in range(nc):
        for e in range(ns):
            if (d, e) in row_copy:
                row_copy[d, e].wait_recv()
        mine = f_ref[...] if d == 0 else row_buf[d, 0]
        near, far = normalize(mine, row_buf[d, 1])
        unit[pl.ds(d * rows, rows), :feats] = near
        unit[pl.ds(d * rows, rows), feats:] = far

    def fold(col_feats, values):
        cosine = lax.dot_general(
            col_feats, unit[...], (((1,), (1,)), ((), ())), preferred_element_type=jnp.float32
        )
        affinity = (1.0 + cosine) * 0.5
        for level in range(POWER.bit_length() - 1):
            affinity = affinity * affinity
        tall = jnp.broadcast_to(values, (128, half)).T[:, :1]
        return (
            jnp.sum(affinity * tall, axis=0, keepdims=True),
            jnp.sum(affinity, axis=0, keepdims=True),
        )

    weighted, degree = fold(unit[own, :], v_ref[:, own])
    for d in sorted(ahead, key=lambda d: min(d, nb - d)):
        for e in range(ns):
            col_copy[d, e].wait_recv()
        val_copy[d].wait_recv()
        near, far = normalize(col_buf[d, 0], col_buf[d, 1])
        more, extra = fold(jnp.concatenate([near, far], axis=1), val_buf[d])
        weighted, degree = weighted + more, degree + extra
    for d in range(nc):
        place = lax.rem(x + d, nc)
        part[place, 0:1, :] = weighted[:, d * rows:(d + 1) * rows]
        part[place, 1:2, :] = degree[:, d * rows:(d + 1) * rows]

    for d, e in plane:
        slot = ((nc - d) % nc, e)
        red_copy[slot] = remote(
            part, red_buf.at[slot], red_send.at[slot], red_recv.at[slot], plane_id(d, e)
        )
    for slot in plane:
        red_copy[slot].wait_recv()

    def gathered(place):
        total = None
        for d in range(nc):
            first = part[place] if d == 0 else red_buf[d, 0, place]
            pair = first + red_buf[d, 1, place]
            total = pair if total is None else total + pair
        return total[0:1, :], total[1:2, :]

    lanes = jnp.zeros((1, 128), jnp.float32)
    for place in range(nc):
        block_weighted, block_degree = gathered(place)
        size = jnp.abs(block_weighted / block_degree)
        for start in range(0, rows, 128):
            lanes = lanes + size[:, start:start + 128]
    tot[...] = lanes
    for d in ahead:
        tot_copy[nb - d] = remote(
            tot, tot_buf.at[nb - d], tot_send.at[nb - d], tot_recv.at[nb - d], line_id(d, 0)
        )
    own_weighted, own_degree = gathered(x)
    averaged = own_weighted / own_degree
    mean_ref[...] = own_degree / points
    for copies in (row_copy, col_copy, val_copy, red_copy):
        for copy in copies.values():
            copy.wait_send()
    for d in ahead:
        tot_copy[d].wait_recv()
        lanes = lanes + tot_buf[d]
    total = jnp.sum(lanes, axis=1, keepdims=True)
    new_ref[...] = averaged / (total / points + 1e-06)
    for copy in tot_copy.values():
        copy.wait_send()


def local(nb, nc, ns, features, vector):
    rows, feats = features.shape
    half = rows // ns
    dma = pltpu.SemaphoreType.DMA
    vmem = pl.BlockSpec(memory_space=pltpu.VMEM)
    new, mean = pl.pallas_call(
        functools.partial(kernel, nb, nc, ns),
        out_shape=(
            jax.ShapeDtypeStruct((1, rows), jnp.float32),
            jax.ShapeDtypeStruct((1, rows), jnp.float32),
        ),
        in_specs=[vmem, vmem],
        out_specs=(vmem, vmem),
        scratch_shapes=[
            pltpu.VMEM((nc, ns, rows, feats), jnp.bfloat16),
            pltpu.VMEM((nb, ns, half, feats), jnp.bfloat16),
            pltpu.VMEM((nb, 1, half), jnp.float32),
            pltpu.VMEM((nc * rows, ns * feats), jnp.bfloat16),
            pltpu.VMEM((nc, 2, rows), jnp.float32),
            pltpu.VMEM((nc, ns, nc, 2, rows), jnp.float32),
            pltpu.VMEM((1, 128), jnp.float32),
            pltpu.VMEM((nb, 1, 128), jnp.float32),
            dma((nc, ns)), dma((nc, ns)),
            dma((nb, ns)), dma((nb, ns)),
            dma((nb,)), dma((nb,)),
            dma((nc, ns)), dma((nc, ns)),
            dma((nb,)), dma((nb,)),
        ],
        compiler_params=pltpu.CompilerParams(collective_id=0, has_side_effects=True),
    )(features, vector.reshape(1, rows))
    return new.reshape(rows), mean.reshape(rows)


def solution(mesh):
    in_specs = (P(("groups", "blk", "cols"), "sub"), P(("groups", "blk", "cols")))
    out_specs = (P(("groups", "blk", "cols")), P(("groups", "blk", "cols")))
    sizes = (mesh.shape["blk"], mesh.shape["cols"], mesh.shape["sub"])
    return jax.shard_map(
        functools.partial(local, *sizes), mesh=mesh, in_specs=in_specs, out_specs=out_specs,
        check_vma=False,
    )
```

```python
import functools
import math

import jax
import jax.numpy as jnp
from jax import lax
from jax.experimental import pallas as pl
from jax.experimental.pallas import tpu as pltpu
from jax.sharding import PartitionSpec as P

POWER = 16
MESH = pl.DeviceIdType.MESH


def normalize(first, second):
    first = first.astype(jnp.float32)
    second = second.astype(jnp.float32)
    width = first.shape[1] + second.shape[1]
    squares = jnp.sum(first * first + second * second, axis=1, keepdims=True)
    scale = lax.rsqrt(squares * (1.0 / width) + 1e-06) * (1.0 / math.sqrt(width))
    return (first * scale).astype(jnp.bfloat16), (second * scale).astype(jnp.bfloat16)


def kernel(
    nb, nc, ns, f_ref, v_ref, new_ref, mean_ref,
    row_buf, col_buf, val_buf, unit, part, all_buf, own_sums,
    row_send, row_recv, col_send, col_recv, val_send, val_recv,
    all_send, all_recv, below_in, above_in,
):
    z, x, c = lax.axis_index("blk"), lax.axis_index("cols"), lax.axis_index("sub")
    rows, feats = f_ref.shape
    half = rows // ns
    points = rows * nb * nc
    plane = [(d, e) for d in range(nc) for e in range(ns) if (d, e) != (0, 0)]
    ahead = list(range(1, nb))

    def plane_id(d, e):
        return {"cols": lax.rem(x + d, nc), "sub": lax.rem(c + e, ns)}

    def line_id(d, e):
        return {"blk": lax.rem(z + d, nb), "sub": lax.rem(c + e, ns)}

    def full_id(dz, d, e):
        return {
            "blk": lax.rem(z + dz, nb), "cols": lax.rem(x + d, nc), "sub": lax.rem(c + e, ns),
        }

    barrier = pltpu.get_barrier_semaphore()
    for cond, d in ((z + 1 < nb, 1), (z >= 1, nb - 1)):
        @pl.when(cond)
        def _():
            for e in range(ns):
                pl.semaphore_signal(barrier, 1, device_id=line_id(d, e), device_id_type=MESH)
    for d, e in plane:
        pl.semaphore_signal(barrier, 1, device_id=plane_id(d, e), device_id_type=MESH)
    beside = jnp.where(z >= 1, ns, 0) + jnp.where(z + 1 < nb, ns, 0)
    pl.semaphore_wait(barrier, len(plane) + beside)

    def remote(src, dst, send, recv, device):
        return pltpu.make_async_remote_copy(
            src_ref=src, dst_ref=dst, send_sem=send, recv_sem=recv,
            device_id=device, device_id_type=MESH,
        )

    row_copy, col_copy, val_copy, all_copy = {}, {}, {}, {}
    own = pl.ds(pl.multiple_of(c * half, half), half)
    for d in ahead:
        val_copy[nb - d] = remote(
            v_ref.at[:, own], val_buf.at[nb - d], val_send.at[nb - d], val_recv.at[nb - d],
            line_id(d, 0),
        )
        for e in range(ns):
            slot = (nb - d, e)
            wanted = pl.ds(pl.multiple_of(lax.rem(c + e, ns) * half, half), half)
            col_copy[slot] = remote(
                f_ref.at[wanted, :], col_buf.at[slot], col_send.at[slot], col_recv.at[slot],
                line_id(d, e),
            )

    def start_line(d):
        for e in range(ns):
            col_copy[nb - d, e].start()
        val_copy[nb - d].start()

    for k in ahead:
        @pl.when(z + k < nb)
        def _():
            if k > 1:
                pl.semaphore_wait(above_in.at[k], 1)
            if k + 1 < nb:
                @pl.when(z >= 1)
                def _():
                    pl.semaphore_signal(
                        above_in.at[k + 1], 1, device_id=line_id(nb - 1, 0), device_id_type=MESH
                    )
            start_line(k)

        @pl.when(z >= k)
        def _():
            if k > 1:
                pl.semaphore_wait(below_in.at[k], 1)
            if k + 1 < nb:
                @pl.when(z + 1 < nb)
                def _():
                    pl.semaphore_signal(
                        below_in.at[k + 1], 1, device_id=line_id(1, 0), device_id_type=MESH
                    )
            start_line(nb - k)

        if k == 1:
            for d, e in plane:
                slot = ((nc - d) % nc, e)
                row_copy[slot] = remote(
                    f_ref, row_buf.at[slot], row_send.at[slot], row_recv.at[slot], plane_id(d, e)
                )
                row_copy[slot].start()

    for d in range(nc):
        for e in range(ns):
            if (d, e) in row_copy:
                row_copy[d, e].wait_recv()
        mine = f_ref[...] if d == 0 else row_buf[d, 0]
        near, far = normalize(mine, row_buf[d, 1])
        place = pl.ds(pl.multiple_of(lax.rem(x + d, nc) * rows, rows), rows)
        unit[place, :feats] = near
        unit[place, feats:] = far

    def fold(col_feats, values):
        cosine = lax.dot_general(
            col_feats, unit[...], (((1,), (1,)), ((), ())), preferred_element_type=jnp.float32
        )
        affinity = (1.0 + cosine) * 0.5
        for level in range(POWER.bit_length() - 1):
            affinity = affinity * affinity
        tall = jnp.broadcast_to(values, (128, half)).T[:, :1]
        return (
            jnp.sum(affinity * tall, axis=0, keepdims=True),
            jnp.sum(affinity, axis=0, keepdims=True),
        )

    own_cols = pl.ds(pl.multiple_of(x * rows + c * half, half), half)
    weighted, degree = fold(unit[own_cols, :], v_ref[:, own])
    for d in sorted(ahead, key=lambda d: min(d, nb - d)):
        for e in range(ns):
            col_copy[d, e].wait_recv()
        val_copy[d].wait_recv()
        near, far = normalize(col_buf[d, 0], col_buf[d, 1])
        more, extra = fold(jnp.concatenate([near, far], axis=1), val_buf[d])
        weighted, degree = weighted + more, degree + extra
    tiles = nc * rows // 128
    for i in range(tiles):
        part[i:i + 1, :] = weighted[:, i * 128:(i + 1) * 128]
        part[tiles + i:tiles + i + 1, :] = degree[:, i * 128:(i + 1) * 128]

    for dz in ahead + [0]:
        for d in range(nc):
            for e in range(ns):
                if (dz, d, e) == (0, 0, 0):
                    continue
                slot = ((nb - dz) % nb, (nc - d) % nc, e)
                all_copy[slot] = remote(
                    part, all_buf.at[slot], all_send.at[slot], all_recv.at[slot],
                    full_id(dz, d, e),
                )
                all_copy[slot].start()
    for copies in (row_copy, col_copy, val_copy):
        for copy in copies.values():
            copy.wait_send()

    sizes = None
    for dz in range(nb):
        total = None
        for d in range(nc):
            for e in range(ns):
                if (dz, d, e) != (0, 0, 0):
                    all_copy[dz, d, e].wait_recv()
            first = part[...] if (dz, d) == (0, 0) else all_buf[dz, d, 0]
            pair = first + all_buf[dz, d, 1]
            total = pair if total is None else total + pair
        averaged = total[:tiles] / total[tiles:]
        if dz == 0:
            own_sums[:tiles] = averaged
            own_sums[tiles:] = total[tiles:]
        size = jnp.abs(averaged)
        sizes = size if sizes is None else sizes + size
    mean = jnp.sum(sizes, axis=(0, 1), keepdims=True) / points + 1e-06
    for i in range(rows // 128):
        lanes = slice(i * 128, (i + 1) * 128)
        first = x * (rows // 128) + i
        new_ref[:, lanes] = own_sums[pl.ds(first, 1), :] / mean
        mean_ref[:, lanes] = own_sums[pl.ds(tiles + first, 1), :] / points
    for copy in all_copy.values():
        copy.wait_send()


def local(nb, nc, ns, features, vector):
    rows, feats = features.shape
    half = rows // ns
    tiles = 2 * nc * rows // 128
    dma = pltpu.SemaphoreType.DMA
    vmem = pl.BlockSpec(memory_space=pltpu.VMEM)
    new, mean = pl.pallas_call(
        functools.partial(kernel, nb, nc, ns),
        out_shape=(
            jax.ShapeDtypeStruct((1, rows), jnp.float32),
            jax.ShapeDtypeStruct((1, rows), jnp.float32),
        ),
        in_specs=[vmem, vmem],
        out_specs=(vmem, vmem),
        scratch_shapes=[
            pltpu.VMEM((nc, ns, rows, feats), jnp.bfloat16),
            pltpu.VMEM((nb, ns, half, feats), jnp.bfloat16),
            pltpu.VMEM((nb, 1, half), jnp.float32),
            pltpu.VMEM((nc * rows, ns * feats), jnp.bfloat16),
            pltpu.VMEM((tiles, 128), jnp.float32),
            pltpu.VMEM((nb, nc, ns, tiles, 128), jnp.float32),
            pltpu.VMEM((tiles, 128), jnp.float32),
            dma((nc, ns)), dma((nc, ns)),
            dma((nb, ns)), dma((nb, ns)),
            dma((nb,)), dma((nb,)),
            dma((nb, nc, ns)), dma((nb, nc, ns)),
            pltpu.SemaphoreType.REGULAR((nb,)), pltpu.SemaphoreType.REGULAR((nb,)),
        ],
        compiler_params=pltpu.CompilerParams(collective_id=0, has_side_effects=True),
    )(features, vector.reshape(1, rows))
    return new.reshape(rows), mean.reshape(rows)


def solution(mesh):
    in_specs = (P(("groups", "blk", "cols"), "sub"), P(("groups", "blk", "cols")))
    out_specs = (P(("groups", "blk", "cols")), P(("groups", "blk", "cols")))
    sizes = (mesh.shape["blk"], mesh.shape["cols"], mesh.shape["sub"])
    return jax.shard_map(
        functools.partial(local, *sizes), mesh=mesh, in_specs=in_specs, out_specs=out_specs,
        check_vma=False,
    )
```

```python
import functools
import math

import jax
import jax.numpy as jnp
from jax import lax
from jax.experimental import pallas as pl
from jax.experimental.pallas import tpu as pltpu
from jax.sharding import PartitionSpec as P

POWER = 16
MESH = pl.DeviceIdType.MESH


def normalize(first, second):
    first = first.astype(jnp.float32)
    second = second.astype(jnp.float32)
    width = first.shape[1] + second.shape[1]
    squares = jnp.sum(first * first + second * second, axis=1, keepdims=True)
    scale = lax.rsqrt(squares * (1.0 / width) + 1e-06) * (1.0 / math.sqrt(width))
    return (first * scale).astype(jnp.bfloat16), (second * scale).astype(jnp.bfloat16)


def kernel(
    nb, nc, ns, f_hbm, v_hbm, new_ref, mean_ref,
    f_ref, v_ref, load_sem,
    row_buf, col_buf, val_buf, unit, part, all_buf, own_sums,
    row_send, row_recv, col_send, col_recv, val_send, val_recv,
    all_send, all_recv, below_in, above_in,
):
    z, x, c = lax.axis_index("blk"), lax.axis_index("cols"), lax.axis_index("sub")
    f_load = pltpu.make_async_copy(f_hbm, f_ref, load_sem.at[0])
    v_load = pltpu.make_async_copy(v_hbm, v_ref, load_sem.at[1])
    f_load.start()
    v_load.start()
    rows, feats = f_ref.shape
    half = rows // ns
    points = rows * nb * nc
    plane = [(d, e) for d in range(nc) for e in range(ns) if (d, e) != (0, 0)]
    ahead = list(range(1, nb))

    def plane_id(d, e):
        return {"cols": lax.rem(x + d, nc), "sub": lax.rem(c + e, ns)}

    def line_id(d, e):
        return {"blk": lax.rem(z + d, nb), "sub": lax.rem(c + e, ns)}

    def full_id(dz, d, e):
        return {
            "blk": lax.rem(z + dz, nb), "cols": lax.rem(x + d, nc), "sub": lax.rem(c + e, ns),
        }

    barrier = pltpu.get_barrier_semaphore()
    for cond, d in ((z + 1 < nb, 1), (z >= 1, nb - 1)):
        @pl.when(cond)
        def _():
            for e in range(ns):
                pl.semaphore_signal(barrier, 1, device_id=line_id(d, e), device_id_type=MESH)
    for d, e in plane:
        pl.semaphore_signal(barrier, 1, device_id=plane_id(d, e), device_id_type=MESH)
    beside = jnp.where(z >= 1, ns, 0) + jnp.where(z + 1 < nb, ns, 0)
    pl.semaphore_wait(barrier, len(plane) + beside)

    f_load.wait()
    v_load.wait()

    def remote(src, dst, send, recv, device):
        return pltpu.make_async_remote_copy(
            src_ref=src, dst_ref=dst, send_sem=send, recv_sem=recv,
            device_id=device, device_id_type=MESH,
        )

    row_copy, col_copy, val_copy, all_copy = {}, {}, {}, {}
    own = pl.ds(pl.multiple_of(c * half, half), half)
    for d in ahead:
        val_copy[nb - d] = remote(
            v_ref.at[:, own], val_buf.at[nb - d], val_send.at[nb - d], val_recv.at[nb - d],
            line_id(d, 0),
        )
        for e in range(ns):
            slot = (nb - d, e)
            wanted = pl.ds(pl.multiple_of(lax.rem(c + e, ns) * half, half), half)
            col_copy[slot] = remote(
                f_ref.at[wanted, :], col_buf.at[slot], col_send.at[slot], col_recv.at[slot],
                line_id(d, e),
            )

    def start_line(d):
        for e in range(ns):
            col_copy[nb - d, e].start()
        val_copy[nb - d].start()

    for d, e in plane:
        slot = ((nc - d) % nc, e)
        row_copy[slot] = remote(
            f_ref, row_buf.at[slot], row_send.at[slot], row_recv.at[slot], plane_id(d, e)
        )
        row_copy[slot].start()

    for k in ahead:
        @pl.when(z + k < nb)
        def _():
            if k > 1:
                pl.semaphore_wait(above_in.at[k], 1)
            if k + 1 < nb:
                @pl.when(z >= 1)
                def _():
                    pl.semaphore_signal(
                        above_in.at[k + 1], 1, device_id=line_id(nb - 1, 0), device_id_type=MESH
                    )
            start_line(k)

        @pl.when(z >= k)
        def _():
            if k > 1:
                pl.semaphore_wait(below_in.at[k], 1)
            if k + 1 < nb:
                @pl.when(z + 1 < nb)
                def _():
                    pl.semaphore_signal(
                        below_in.at[k + 1], 1, device_id=line_id(1, 0), device_id_type=MESH
                    )
            start_line(nb - k)

    for d in range(nc):
        for e in range(ns):
            if (d, e) in row_copy:
                row_copy[d, e].wait_recv()
        mine = f_ref[...] if d == 0 else row_buf[d, 0]
        near, far = normalize(mine, row_buf[d, 1])
        place = pl.ds(pl.multiple_of(lax.rem(x + d, nc) * rows, rows), rows)
        unit[place, :feats] = near
        unit[place, feats:] = far

    def fold(col_feats, values):
        cosine = lax.dot_general(
            col_feats, unit[...], (((1,), (1,)), ((), ())), preferred_element_type=jnp.float32
        )
        affinity = (1.0 + cosine) * 0.5
        for level in range(POWER.bit_length() - 1):
            affinity = affinity * affinity
        tall = jnp.broadcast_to(values, (128, half)).T[:, :1]
        return (
            jnp.sum(affinity * tall, axis=0, keepdims=True),
            jnp.sum(affinity, axis=0, keepdims=True),
        )

    own_cols = pl.ds(pl.multiple_of(x * rows + c * half, half), half)
    weighted, degree = fold(unit[own_cols, :], v_ref[:, own])
    for d in sorted(ahead, key=lambda d: min(d, nb - d)):
        for e in range(ns):
            col_copy[d, e].wait_recv()
        val_copy[d].wait_recv()
        near, far = normalize(col_buf[d, 0], col_buf[d, 1])
        more, extra = fold(jnp.concatenate([near, far], axis=1), val_buf[d])
        weighted, degree = weighted + more, degree + extra
    tiles = nc * rows // 128
    for i in range(tiles):
        part[i:i + 1, :] = weighted[:, i * 128:(i + 1) * 128]
        part[tiles + i:tiles + i + 1, :] = degree[:, i * 128:(i + 1) * 128]

    for dz in [0] + ahead:
        for d in range(nc):
            for e in range(ns):
                if (dz, d, e) == (0, 0, 0):
                    continue
                slot = ((nb - dz) % nb, (nc - d) % nc, e)
                all_copy[slot] = remote(
                    part, all_buf.at[slot], all_send.at[slot], all_recv.at[slot],
                    full_id(dz, d, e),
                )
                all_copy[slot].start()
    for copies in (row_copy, col_copy, val_copy):
        for copy in copies.values():
            copy.wait_send()

    sizes = None
    for dz in range(nb):
        total = None
        for d in range(nc):
            for e in range(ns):
                if (dz, d, e) != (0, 0, 0):
                    all_copy[dz, d, e].wait_recv()
            first = part[...] if (dz, d) == (0, 0) else all_buf[dz, d, 0]
            pair = first + all_buf[dz, d, 1]
            total = pair if total is None else total + pair
        averaged = total[:tiles] / total[tiles:]
        if dz == 0:
            own_sums[:tiles] = averaged
            own_sums[tiles:] = total[tiles:]
        size = jnp.abs(averaged)
        sizes = size if sizes is None else sizes + size
    mean = jnp.sum(sizes, axis=(0, 1), keepdims=True) / points + 1e-06
    for i in range(rows // 128):
        lanes = slice(i * 128, (i + 1) * 128)
        first = x * (rows // 128) + i
        new_ref[0:1, lanes] = own_sums[pl.ds(first, 1), :]
        new_ref[1:2, lanes] = own_sums[pl.ds(tiles + first, 1), :]
    mean_ref[...] = jnp.broadcast_to(mean, mean_ref.shape)
    for copy in all_copy.values():
        copy.wait_send()


def local(nb, nc, ns, features, vector):
    rows, feats = features.shape
    half = rows // ns
    tiles = 2 * nc * rows // 128
    dma = pltpu.SemaphoreType.DMA
    vmem = pl.BlockSpec(memory_space=pltpu.VMEM)
    new, mean = pl.pallas_call(
        functools.partial(kernel, nb, nc, ns),
        out_shape=(
            jax.ShapeDtypeStruct((2, rows), jnp.float32),
            jax.ShapeDtypeStruct((1, 128), jnp.float32),
        ),
        in_specs=[pl.BlockSpec(memory_space=pl.ANY)] * 2,
        out_specs=(vmem, vmem),
        scratch_shapes=[
            pltpu.VMEM((rows, feats), jnp.bfloat16),
            pltpu.VMEM((1, rows), jnp.float32),
            dma((2,)),
            pltpu.VMEM((nc, ns, rows, feats), jnp.bfloat16),
            pltpu.VMEM((nb, ns, half, feats), jnp.bfloat16),
            pltpu.VMEM((nb, 1, half), jnp.float32),
            pltpu.VMEM((nc * rows, ns * feats), jnp.bfloat16),
            pltpu.VMEM((tiles, 128), jnp.float32),
            pltpu.VMEM((nb, nc, ns, tiles, 128), jnp.float32),
            pltpu.VMEM((tiles, 128), jnp.float32),
            dma((nc, ns)), dma((nc, ns)),
            dma((nb, ns)), dma((nb, ns)),
            dma((nb,)), dma((nb,)),
            dma((nb, nc, ns)), dma((nb, nc, ns)),
            pltpu.SemaphoreType.REGULAR((nb,)), pltpu.SemaphoreType.REGULAR((nb,)),
        ],
        compiler_params=pltpu.CompilerParams(collective_id=0, has_side_effects=True),
    )(features, vector.reshape(1, rows))
    points = rows * nb * nc
    return new[0] / mean[0, 0], new[1] / points


def solution(mesh):
    in_specs = (P(("groups", "blk", "cols"), "sub"), P(("groups", "blk", "cols")))
    out_specs = (P(("groups", "blk", "cols")), P(("groups", "blk", "cols")))
    sizes = (mesh.shape["blk"], mesh.shape["cols"], mesh.shape["sub"])
    return jax.shard_map(
        functools.partial(local, *sizes), mesh=mesh, in_specs=in_specs, out_specs=out_specs,
        check_vma=False,
    )
```

```python
import functools
import math

import jax
import jax.numpy as jnp
from jax import lax
from jax.experimental import pallas as pl
from jax.experimental.pallas import tpu as pltpu
from jax.sharding import PartitionSpec as P

POWER = 16
MESH = pl.DeviceIdType.MESH


def normalize(first, second):
    first = first.astype(jnp.float32)
    second = second.astype(jnp.float32)
    width = first.shape[1] + second.shape[1]
    squares = jnp.sum(first * first + second * second, axis=1, keepdims=True)
    scale = lax.rsqrt(squares * (1.0 / width) + 1e-06) * (1.0 / math.sqrt(width))
    return (first * scale).astype(jnp.bfloat16), (second * scale).astype(jnp.bfloat16)


def kernel(
    nb, nc, ns, f_hbm, v_hbm, new_ref,
    f_ref, v_ref, load_sem,
    row_buf, col_buf, val_buf, unit, part, all_buf, own_sums,
    row_send, row_recv, col_send, col_recv, val_send, val_recv,
    all_send, all_recv, below_in, above_in,
):
    z, x, c = lax.axis_index("blk"), lax.axis_index("cols"), lax.axis_index("sub")
    f_load = pltpu.make_async_copy(f_hbm, f_ref, load_sem.at[0])
    v_load = pltpu.make_async_copy(v_hbm, v_ref, load_sem.at[1])
    f_load.start()
    v_load.start()
    rows, feats = f_ref.shape
    half = rows // ns
    points = rows * nb * nc
    plane = [(d, e) for d in range(nc) for e in range(ns) if (d, e) != (0, 0)]
    ahead = list(range(1, nb))

    def plane_id(d, e):
        return {"cols": lax.rem(x + d, nc), "sub": lax.rem(c + e, ns)}

    def line_id(d, e):
        return {"blk": lax.rem(z + d, nb), "sub": lax.rem(c + e, ns)}

    def full_id(dz, d, e):
        return {
            "blk": lax.rem(z + dz, nb), "cols": lax.rem(x + d, nc), "sub": lax.rem(c + e, ns),
        }

    barrier = pltpu.get_barrier_semaphore()
    for cond, d in ((z + 1 < nb, 1), (z >= 1, nb - 1)):
        @pl.when(cond)
        def _():
            for e in range(ns):
                pl.semaphore_signal(barrier, 1, device_id=line_id(d, e), device_id_type=MESH)
    for d, e in plane:
        pl.semaphore_signal(barrier, 1, device_id=plane_id(d, e), device_id_type=MESH)
    beside = jnp.where(z >= 1, ns, 0) + jnp.where(z + 1 < nb, ns, 0)
    pl.semaphore_wait(barrier, len(plane) + beside)

    f_load.wait()
    v_load.wait()

    def remote(src, dst, send, recv, device):
        return pltpu.make_async_remote_copy(
            src_ref=src, dst_ref=dst, send_sem=send, recv_sem=recv,
            device_id=device, device_id_type=MESH,
        )

    row_copy, col_copy, val_copy, all_copy = {}, {}, {}, {}
    own = pl.ds(pl.multiple_of(c * half, half), half)
    for d in ahead:
        val_copy[nb - d] = remote(
            v_ref.at[:, own], val_buf.at[nb - d], val_send.at[nb - d], val_recv.at[nb - d],
            line_id(d, 0),
        )
        for e in range(ns):
            slot = (nb - d, e)
            wanted = pl.ds(pl.multiple_of(lax.rem(c + e, ns) * half, half), half)
            col_copy[slot] = remote(
                f_ref.at[wanted, :], col_buf.at[slot], col_send.at[slot], col_recv.at[slot],
                line_id(d, e),
            )

    def start_line(d):
        for e in range(ns):
            col_copy[nb - d, e].start()
        val_copy[nb - d].start()

    for d, e in plane:
        slot = ((nc - d) % nc, e)
        row_copy[slot] = remote(
            f_ref, row_buf.at[slot], row_send.at[slot], row_recv.at[slot], plane_id(d, e)
        )
        row_copy[slot].start()

    for k in ahead:
        @pl.when(z + k < nb)
        def _():
            if k > 1:
                pl.semaphore_wait(above_in.at[k], 1)
            if k + 1 < nb:
                @pl.when(z >= 1)
                def _():
                    pl.semaphore_signal(
                        above_in.at[k + 1], 1, device_id=line_id(nb - 1, 0), device_id_type=MESH
                    )
            start_line(k)

        @pl.when(z >= k)
        def _():
            if k > 1:
                pl.semaphore_wait(below_in.at[k], 1)
            if k + 1 < nb:
                @pl.when(z + 1 < nb)
                def _():
                    pl.semaphore_signal(
                        below_in.at[k + 1], 1, device_id=line_id(1, 0), device_id_type=MESH
                    )
            start_line(nb - k)

    for d in range(nc):
        for e in range(ns):
            if (d, e) in row_copy:
                row_copy[d, e].wait_recv()
        mine = f_ref[...] if d == 0 else row_buf[d, 0]
        near, far = normalize(mine, row_buf[d, 1])
        place = pl.ds(pl.multiple_of(lax.rem(x + d, nc) * rows, rows), rows)
        unit[place, :feats] = near
        unit[place, feats:] = far

    def fold(col_feats, values):
        cosine = lax.dot_general(
            col_feats, unit[...], (((1,), (1,)), ((), ())), preferred_element_type=jnp.float32
        )
        affinity = (1.0 + cosine) * 0.5
        for level in range(POWER.bit_length() - 1):
            affinity = affinity * affinity
        tall = jnp.broadcast_to(values, (128, half)).T[:, :1]
        return (
            jnp.sum(affinity * tall, axis=0, keepdims=True),
            jnp.sum(affinity, axis=0, keepdims=True),
        )

    own_cols = pl.ds(pl.multiple_of(x * rows + c * half, half), half)
    weighted, degree = fold(unit[own_cols, :], v_ref[:, own])
    for d in sorted(ahead, key=lambda d: min(d, nb - d)):
        for e in range(ns):
            col_copy[d, e].wait_recv()
        val_copy[d].wait_recv()
        near, far = normalize(col_buf[d, 0], col_buf[d, 1])
        more, extra = fold(jnp.concatenate([near, far], axis=1), val_buf[d])
        weighted, degree = weighted + more, degree + extra
    tiles = nc * rows // 128
    for i in range(tiles):
        part[i:i + 1, :] = weighted[:, i * 128:(i + 1) * 128]
        part[tiles + i:tiles + i + 1, :] = degree[:, i * 128:(i + 1) * 128]

    for dz in [0] + ahead:
        for d in range(nc):
            for e in range(ns):
                if (dz, d, e) == (0, 0, 0):
                    continue
                slot = ((nb - dz) % nb, (nc - d) % nc, e)
                all_copy[slot] = remote(
                    part, all_buf.at[slot], all_send.at[slot], all_recv.at[slot],
                    full_id(dz, d, e),
                )
                all_copy[slot].start()
    for copies in (row_copy, col_copy, val_copy):
        for copy in copies.values():
            copy.wait_send()

    sizes = None
    for dz in range(nb):
        total = None
        for d in range(nc):
            for e in range(ns):
                if (dz, d, e) != (0, 0, 0):
                    all_copy[dz, d, e].wait_recv()
            first = part[...] if (dz, d) == (0, 0) else all_buf[dz, d, 0]
            pair = first + all_buf[dz, d, 1]
            total = pair if total is None else total + pair
        averaged = total[:tiles] / total[tiles:]
        if dz == 0:
            own_sums[:tiles] = averaged
            own_sums[tiles:] = total[tiles:]
        size = jnp.abs(averaged)
        sizes = size if sizes is None else sizes + size
    mean = jnp.sum(sizes, axis=(0, 1), keepdims=True) / points + 1e-06
    for i in range(rows // 128):
        lanes = slice(i * 128, (i + 1) * 128)
        first = x * (rows // 128) + i
        new_ref[0:1, lanes] = own_sums[pl.ds(first, 1), :]
        new_ref[1:2, lanes] = own_sums[pl.ds(tiles + first, 1), :]
    new_ref[2:3, :] = jnp.broadcast_to(mean, (1, rows))
    for copy in all_copy.values():
        copy.wait_send()


def local(nb, nc, ns, features, vector):
    rows, feats = features.shape
    half = rows // ns
    tiles = 2 * nc * rows // 128
    dma = pltpu.SemaphoreType.DMA
    vmem = pl.BlockSpec(memory_space=pltpu.VMEM)
    sums = pl.pallas_call(
        functools.partial(kernel, nb, nc, ns),
        out_shape=pltpu.VMEM((3, rows), jnp.float32),
        in_specs=[pl.BlockSpec(memory_space=pl.ANY)] * 2,
        out_specs=vmem,
        scratch_shapes=[
            pltpu.VMEM((rows, feats), jnp.bfloat16),
            pltpu.VMEM((1, rows), jnp.float32),
            dma((2,)),
            pltpu.VMEM((nc, ns, rows, feats), jnp.bfloat16),
            pltpu.VMEM((nb, ns, half, feats), jnp.bfloat16),
            pltpu.VMEM((nb, 1, half), jnp.float32),
            pltpu.VMEM((nc * rows, ns * feats), jnp.bfloat16),
            pltpu.VMEM((tiles, 128), jnp.float32),
            pltpu.VMEM((nb, nc, ns, tiles, 128), jnp.float32),
            pltpu.VMEM((tiles, 128), jnp.float32),
            dma((nc, ns)), dma((nc, ns)),
            dma((nb, ns)), dma((nb, ns)),
            dma((nb,)), dma((nb,)),
            dma((nb, nc, ns)), dma((nb, nc, ns)),
            pltpu.SemaphoreType.REGULAR((nb,)), pltpu.SemaphoreType.REGULAR((nb,)),
        ],
        compiler_params=pltpu.CompilerParams(collective_id=0, has_side_effects=True),
    )(features, vector.reshape(1, rows))
    points = rows * nb * nc
    return sums[0] / sums[2], sums[1] / points


def solution(mesh):
    in_specs = (P(("groups", "blk", "cols"), "sub"), P(("groups", "blk", "cols")))
    out_specs = (P(("groups", "blk", "cols")), P(("groups", "blk", "cols")))
    sizes = (mesh.shape["blk"], mesh.shape["cols"], mesh.shape["sub"])
    return jax.shard_map(
        functools.partial(local, *sizes), mesh=mesh, in_specs=in_specs, out_specs=out_specs,
        check_vma=False,
    )
```

```python
import functools
import math

import jax
import jax.numpy as jnp
from jax import lax
from jax.experimental import pallas as pl
from jax.experimental.pallas import tpu as pltpu
from jax.sharding import PartitionSpec as P

POWER = 16
MESH = pl.DeviceIdType.MESH


def normalize(first, second):
    first = first.astype(jnp.float32)
    second = second.astype(jnp.float32)
    width = first.shape[1] + second.shape[1]
    squares = jnp.sum(first * first + second * second, axis=1, keepdims=True)
    scale = lax.rsqrt(squares * (1.0 / width) + 1e-06) * (1.0 / math.sqrt(width))
    return (first * scale).astype(jnp.bfloat16), (second * scale).astype(jnp.bfloat16)


def kernel(
    nb, nc, ns, f_hbm, v_hbm, new_ref,
    f_ref, v_ref, load_sem,
    row_buf, col_buf, val_buf, unit, part, all_buf, own_sums,
    row_send, row_recv, col_send, col_recv, val_send, val_recv,
    all_send, all_recv, below_in, above_in,
):
    z, x, c = lax.axis_index("blk"), lax.axis_index("cols"), lax.axis_index("sub")
    f_load = pltpu.make_async_copy(f_hbm, f_ref, load_sem.at[0])
    v_load = pltpu.make_async_copy(v_hbm, v_ref, load_sem.at[1])
    f_load.start()
    v_load.start()
    rows, feats = f_ref.shape
    half = rows // ns
    points = rows * nb * nc
    plane = [(d, e) for d in range(nc) for e in range(ns) if (d, e) != (0, 0)]
    ahead = list(range(1, nb))

    def plane_id(d, e):
        return {"cols": lax.rem(x + d, nc), "sub": lax.rem(c + e, ns)}

    def line_id(d, e):
        return {"blk": lax.rem(z + d, nb), "sub": lax.rem(c + e, ns)}

    def full_id(dz, d, e):
        return {
            "blk": lax.rem(z + dz, nb), "cols": lax.rem(x + d, nc), "sub": lax.rem(c + e, ns),
        }

    barrier = pltpu.get_barrier_semaphore()
    for cond, d in ((z + 1 < nb, 1), (z >= 1, nb - 1)):
        @pl.when(cond)
        def _():
            for e in range(ns):
                pl.semaphore_signal(barrier, 1, device_id=line_id(d, e), device_id_type=MESH)
    for d, e in plane:
        pl.semaphore_signal(barrier, 1, device_id=plane_id(d, e), device_id_type=MESH)
    beside = jnp.where(z >= 1, ns, 0) + jnp.where(z + 1 < nb, ns, 0)
    pl.semaphore_wait(barrier, len(plane) + beside)

    f_load.wait()
    v_load.wait()

    def remote(src, dst, send, recv, device):
        return pltpu.make_async_remote_copy(
            src_ref=src, dst_ref=dst, send_sem=send, recv_sem=recv,
            device_id=device, device_id_type=MESH,
        )

    row_copy, col_copy, val_copy, all_copy = {}, {}, {}, {}
    own = pl.ds(pl.multiple_of(c * half, half), half)
    for d in ahead:
        val_copy[nb - d] = remote(
            v_ref.at[:, own], val_buf.at[nb - d], val_send.at[nb - d], val_recv.at[nb - d],
            line_id(d, 0),
        )
        for e in range(ns):
            slot = (nb - d, e)
            wanted = pl.ds(pl.multiple_of(lax.rem(c + e, ns) * half, half), half)
            col_copy[slot] = remote(
                f_ref.at[wanted, :], col_buf.at[slot], col_send.at[slot], col_recv.at[slot],
                line_id(d, e),
            )

    def start_line(d):
        for e in range(ns):
            col_copy[nb - d, e].start()
        val_copy[nb - d].start()

    for d, e in plane:
        slot = ((nc - d) % nc, e)
        row_copy[slot] = remote(
            f_ref, row_buf.at[slot], row_send.at[slot], row_recv.at[slot], plane_id(d, e)
        )
        row_copy[slot].start()

    for k in ahead:
        @pl.when(z + k < nb)
        def _():
            if k > 1:
                pl.semaphore_wait(above_in.at[k], 1)
            if k + 1 < nb:
                @pl.when(z >= 1)
                def _():
                    pl.semaphore_signal(
                        above_in.at[k + 1], 1, device_id=line_id(nb - 1, 0), device_id_type=MESH
                    )
            start_line(k)

        @pl.when(z >= k)
        def _():
            if k > 1:
                pl.semaphore_wait(below_in.at[k], 1)
            if k + 1 < nb:
                @pl.when(z + 1 < nb)
                def _():
                    pl.semaphore_signal(
                        below_in.at[k + 1], 1, device_id=line_id(1, 0), device_id_type=MESH
                    )
            start_line(nb - k)

    for d in range(nc):
        for e in range(ns):
            if (d, e) in row_copy:
                row_copy[d, e].wait_recv()
        mine = f_ref[...] if d == 0 else row_buf[d, 0]
        near, far = normalize(mine, row_buf[d, 1])
        place = pl.ds(pl.multiple_of(lax.rem(x + d, nc) * rows, rows), rows)
        unit[place, :feats] = near
        unit[place, feats:] = far

    def fold(col_feats, values):
        cosine = lax.dot_general(
            col_feats, unit[...], (((1,), (1,)), ((), ())), preferred_element_type=jnp.float32
        )
        affinity = (1.0 + cosine) * 0.5
        for level in range(POWER.bit_length() - 1):
            affinity = affinity * affinity
        tall = jnp.broadcast_to(values, (128, half)).T[:, :1]
        return (
            jnp.sum(affinity * tall, axis=0, keepdims=True),
            jnp.sum(affinity, axis=0, keepdims=True),
        )

    own_cols = pl.ds(pl.multiple_of(x * rows + c * half, half), half)
    weighted, degree = fold(unit[own_cols, :], v_ref[:, own])
    for d in sorted(ahead, key=lambda d: min(d, nb - d)):
        for e in range(ns):
            col_copy[d, e].wait_recv()
        val_copy[d].wait_recv()
        near, far = normalize(col_buf[d, 0], col_buf[d, 1])
        more, extra = fold(jnp.concatenate([near, far], axis=1), val_buf[d])
        weighted, degree = weighted + more, degree + extra
    tiles = nc * rows // 128
    for i in range(tiles):
        part[i:i + 1, :] = weighted[:, i * 128:(i + 1) * 128]
        part[tiles + i:tiles + i + 1, :] = degree[:, i * 128:(i + 1) * 128]

    for dz in range(nb):
        for d in range(nc):
            for e in range(ns):
                if (dz, d, e) == (0, 0, 0):
                    continue
                slot = ((nb - dz) % nb, (nc - d) % nc, e)
                all_copy[slot] = remote(
                    part, all_buf.at[slot], all_send.at[slot], all_recv.at[slot],
                    full_id(dz, d, e),
                )

    def spread(dz):
        for d in range(nc):
            for e in range(ns):
                if (dz, d, e) != (0, 0, 0):
                    all_copy[(nb - dz) % nb, (nc - d) % nc, e].start()

    for k in reversed(ahead):
        @pl.when(z + k < nb)
        def _():
            spread(k)

        @pl.when(z >= k)
        def _():
            spread(nb - k)
    spread(0)
    for copies in (row_copy, col_copy, val_copy):
        for copy in copies.values():
            copy.wait_send()

    sizes = None
    for dz in range(nb):
        total = None
        for d in range(nc):
            for e in range(ns):
                if (dz, d, e) != (0, 0, 0):
                    all_copy[dz, d, e].wait_recv()
            first = part[...] if (dz, d) == (0, 0) else all_buf[dz, d, 0]
            pair = first + all_buf[dz, d, 1]
            total = pair if total is None else total + pair
        averaged = total[:tiles] / total[tiles:]
        if dz == 0:
            own_sums[:tiles] = averaged
            own_sums[tiles:] = total[tiles:]
        size = jnp.abs(averaged)
        sizes = size if sizes is None else sizes + size
    mean = jnp.sum(sizes, axis=(0, 1), keepdims=True) / points + 1e-06
    for i in range(rows // 128):
        lanes = slice(i * 128, (i + 1) * 128)
        first = x * (rows // 128) + i
        new_ref[0:1, lanes] = own_sums[pl.ds(first, 1), :]
        new_ref[1:2, lanes] = own_sums[pl.ds(tiles + first, 1), :]
    new_ref[2:3, :] = jnp.broadcast_to(mean, (1, rows))
    for copy in all_copy.values():
        copy.wait_send()


def local(nb, nc, ns, features, vector):
    rows, feats = features.shape
    half = rows // ns
    tiles = 2 * nc * rows // 128
    dma = pltpu.SemaphoreType.DMA
    vmem = pl.BlockSpec(memory_space=pltpu.VMEM)
    sums = pl.pallas_call(
        functools.partial(kernel, nb, nc, ns),
        out_shape=pltpu.VMEM((3, rows), jnp.float32),
        in_specs=[pl.BlockSpec(memory_space=pl.ANY)] * 2,
        out_specs=vmem,
        scratch_shapes=[
            pltpu.VMEM((rows, feats), jnp.bfloat16),
            pltpu.VMEM((1, rows), jnp.float32),
            dma((2,)),
            pltpu.VMEM((nc, ns, rows, feats), jnp.bfloat16),
            pltpu.VMEM((nb, ns, half, feats), jnp.bfloat16),
            pltpu.VMEM((nb, 1, half), jnp.float32),
            pltpu.VMEM((nc * rows, ns * feats), jnp.bfloat16),
            pltpu.VMEM((tiles, 128), jnp.float32),
            pltpu.VMEM((nb, nc, ns, tiles, 128), jnp.float32),
            pltpu.VMEM((tiles, 128), jnp.float32),
            dma((nc, ns)), dma((nc, ns)),
            dma((nb, ns)), dma((nb, ns)),
            dma((nb,)), dma((nb,)),
            dma((nb, nc, ns)), dma((nb, nc, ns)),
            pltpu.SemaphoreType.REGULAR((nb,)), pltpu.SemaphoreType.REGULAR((nb,)),
        ],
        compiler_params=pltpu.CompilerParams(collective_id=0, has_side_effects=True),
    )(features, vector.reshape(1, rows))
    points = rows * nb * nc
    return sums[0] / sums[2], sums[1] / points


def solution(mesh):
    in_specs = (P(("groups", "blk", "cols"), "sub"), P(("groups", "blk", "cols")))
    out_specs = (P(("groups", "blk", "cols")), P(("groups", "blk", "cols")))
    sizes = (mesh.shape["blk"], mesh.shape["cols"], mesh.shape["sub"])
    return jax.shard_map(
        functools.partial(local, *sizes), mesh=mesh, in_specs=in_specs, out_specs=out_specs,
        check_vma=False,
    )
```
